32 devices in a mesh: parts: 2 (over x), seq: 8 (over z, y), joint: 2 (over core).
Axes of the slice: x: 2, y: 2, z: 4, core: 2. Of those that a mesh axis runs over, the one named last changes fastest.
Arguments:
- motion: bfloat16 [2048, 2, 1024], P(('parts', 'seq', 'joint')), parts along dimension 0, may hold values from -6 to 6
- s_gain: float32 [1024], replicated, may hold values from 0.25 to 1.75
- s_query: bfloat16 [1024, 1024], replicated, may hold values from -4 to 4
- s_key_value: bfloat16 [1024, 2, 1024], replicated, may hold values from -0.25 to 0.25
- s_out: bfloat16 [1024, 1024], replicated, may hold values from -0.375 to 0.375
- t_gain: float32 [1024], replicated, may hold values from 0.25 to 1.75
- t_query: bfloat16 [1024, 1024], P(None, 'joint'), may hold values from -4 to 4
- t_key_value: bfloat16 [1024, 2, 1024], P(None, None, 'joint'), may hold values from -0.25 to 0.25
- t_out: bfloat16 [1024, 1024], P('joint'), may hold values from -0.75 to 0.75
- lengths: int32 [16], P('parts'), parts along dimension 0, may hold values from 1 to 512, 1024 in all
Outputs:
- spatial_out: bfloat16 [2048, 2, 1024], P(('parts', 'seq', 'joint')), parts along dimension 0
- temporal_branch: bfloat16 [2048, 2, 1024], P(('parts', 'seq'), 'joint'), parts along dimension 0
The draws below stay inside these ranges and needn't reach their ends.
There are 2 independent parts, one for each index of `parts`. The reference program is written for one: setup_inputs(seed, part) draws one part's arguments, and reference() takes and returns one part's arrays. A program takes and returns all parts, laid end to end along the dimension named above; an argument that names none is the same for every part. Nothing has to cross between parts.
Inputs may be any that keep to these rules, and one draw needn't show every extreme that they name: clip lengths sum to 1024; the longest clip has exactly 512 frames.
All inputs are finite; a program needn't handle non-finite values.
Results may differ from the reference program's by a relative error of at most 0.014.
Values may be sent and summed in bfloat16 or wider, within the bound.
A program may use at most 128 MiB of HBM per device.

```python
import math
import jax
import jax.numpy as jnp
import numpy as np
from jax import lax

D = 1024
HEADS = 16
HEAD = 64
JOINTS = 2
CLIPS = 8
FRAMES = 1024


def key_columns(key, salt):
    return jnp.clip(jax.random.normal(jax.random.fold_in(key, salt), (D, D), jnp.float32) / math.sqrt(D), -0.25, 0.25)


def value_columns(key, salt):
    return jnp.clip(jax.random.normal(jax.random.fold_in(key, salt), (D, D), jnp.float32) / math.sqrt(D), -0.25, 0.25)


def query_columns(key, salt_fresh):
    fresh = jnp.clip(jax.random.normal(jax.random.fold_in(key, salt_fresh), (D, D), jnp.float32) / math.sqrt(D), -0.25, 0.25)
    return fresh


def draw_s_query(key, part):
    return query_columns(key, 31).astype(jnp.bfloat16)


def draw_s_key_value(key, part):
    return jnp.stack([key_columns(key, 11), value_columns(key, 21)], axis=1).astype(jnp.bfloat16)


def draw_t_query(key, part):
    return query_columns(key, 41).astype(jnp.bfloat16)


def draw_t_key_value(key, part):
    return jnp.stack([key_columns(key, 12), value_columns(key, 22)], axis=1).astype(jnp.bfloat16)


def level_of(rng, extent, pieces, least, top_value):
    loudness = 1.0
    for axis_at, blocks in pieces:
        heights = jax.random.uniform(jax.random.fold_in(jax.random.fold_in(rng, 6), axis_at), (blocks,), jnp.float32, least / len(pieces), top_value / len(pieces))
        loudness = loudness * jnp.repeat(jnp.exp(heights), extent[axis_at] // blocks).reshape((-1,) + (1,) * (len(extent) - 1 - axis_at))
    return loudness


def length_profile(count, total, limit, lean):
    portions = [(1 << 20) // math.isqrt(rank ** lean) + 1 for rank in range(2, count + 1)]
    rest, given = total - limit - (count - 1), [1] * (count - 1)
    while rest > 0:
        movable = [i for i in range(count - 1) if given[i] < limit]
        pool, remaining = sum([portions[i] for i in movable]), rest
        for i in movable:
            more = min(limit - given[i], max(1, remaining * portions[i] // pool), rest)
            given[i] = given[i] + more
            rest = rest - more
    return np.array([limit] + given)


def uneven(stream_key, amount, total, bound, slope):
    if amount == 2:
        one = jax.random.randint(stream_key, (), max(1, total - bound), min(bound, total - 1) + 1)
        return jnp.stack([one, total - one])
    sizes = jnp.asarray(length_profile(amount, total, bound, slope), jnp.int32)
    pairs = (amount - 1) // 2
    giver, sink = sizes[1:1 + 2 * pairs:2], sizes[2:2 + 2 * pairs:2]
    margin = jnp.minimum(giver - 1, bound - sink)
    shifted = jax.random.randint(jax.random.fold_in(stream_key, 1), (pairs,), 0, 1 << 20) % (margin + 1)
    sizes = sizes.at[1:1 + 2 * pairs:2].set(giver - shifted).at[2:2 + 2 * pairs:2].set(sink + shifted)
    return sizes[jax.random.permutation(jax.random.fold_in(stream_key, 2), amount)]


def scatter_about(own_key, extent, scale, bound, split=(), held_as=jnp.bfloat16):
    array = scale * jax.random.normal(own_key, extent, jnp.float32)
    if split:
        array = array * level_of(own_key, extent, split, -0.22, 0.18)
    return jnp.clip(array, -bound, bound).astype(held_as)


def setup_inputs(seed: int = 0, part: int = 0) -> dict:
    streams_of = jax.random.split(jax.random.key(seed), 11)
    part_keys = jax.random.split(jax.random.fold_in(streams_of[10], part), 11)
    return {
        "motion": scatter_about(part_keys[0], (FRAMES, JOINTS, D), 1.0, 6.0, ((0, 16),)),
        "s_gain": jnp.clip(1.0 + 0.15 * jax.random.normal(streams_of[1], (D,), jnp.float32), 0.25, 1.75),
        "s_query": draw_s_query(jax.random.fold_in(streams_of[10], 71), part),
        "s_key_value": draw_s_key_value(jax.random.fold_in(streams_of[10], 71), part),
        "s_out": scatter_about(streams_of[4], (D, D), (D // 4) ** -0.5, 0.375),
        "t_gain": jnp.clip(1.0 + 0.15 * jax.random.normal(streams_of[5], (D,), jnp.float32), 0.25, 1.75),
        "t_query": draw_t_query(jax.random.fold_in(streams_of[10], 71), part),
        "t_key_value": draw_t_key_value(jax.random.fold_in(streams_of[10], 71), part),
        "t_out": scatter_about(streams_of[8], (D, D), (D // 16) ** -0.5, 0.75, ((0, 2),)),
        "lengths": uneven(part_keys[9], CLIPS, FRAMES, FRAMES // 2, 2).astype(jnp.int32),
    }


def layer_norm(values, gain):
    wide = values.astype(jnp.float32)
    mean = lax.optimization_barrier(jnp.mean(wide, axis=-1, keepdims=True))
    spread = lax.optimization_barrier(jnp.mean((wide - mean) * (wide - mean), axis=-1, keepdims=True))
    return ((wide - mean) * lax.rsqrt(spread + 1e-05) * gain).astype(jnp.bfloat16)

def spatial_block(motion, s_gain, s_query, s_key_value, s_out):
    frames, joints, width = motion.shape
    normed = layer_norm(motion, s_gain).reshape(frames * joints, width)
    queries = jnp.dot(normed, s_query, preferred_element_type=jnp.float32).astype(jnp.bfloat16)
    queries = queries.reshape(frames, joints, HEADS, HEAD)
    pairs = jnp.dot(normed, s_key_value.reshape(width, 2 * width), preferred_element_type=jnp.float32).astype(jnp.bfloat16)
    pairs = pairs.reshape(frames, joints, 2, HEADS, HEAD)
    scores = jnp.einsum('fjhe,fkhe->fhjk', queries, pairs[:, :, 0], preferred_element_type=jnp.float32) / jnp.sqrt(jnp.float32(HEAD))
    peak = lax.optimization_barrier(jnp.max(scores, axis=-1, keepdims=True))
    weights = jnp.exp(scores - peak)
    total = lax.optimization_barrier(jnp.sum(weights, axis=-1))
    mixed = jnp.einsum('fhjk,fkhe->fjhe', weights.astype(jnp.bfloat16), pairs[:, :, 1], preferred_element_type=jnp.float32)
    context = (mixed / jnp.transpose(total, (0, 2, 1))[..., None]).astype(jnp.bfloat16)
    context = context.reshape(frames * joints, width)
    update = jnp.dot(context, s_out, preferred_element_type=jnp.float32).reshape(frames, joints, width)
    return (motion.astype(jnp.float32) + update).astype(jnp.bfloat16)

def clip_index(frame_ids, lengths):
    ends = jnp.cumsum(lengths).astype(jnp.int32)
    return lax.optimization_barrier(jnp.sum((frame_ids[:, None] >= ends[None, :]).astype(jnp.int32), axis=1)).astype(jnp.int32)

def reference(motion, s_gain, s_query, s_key_value, s_out, t_gain, t_query, t_key_value, t_out, lengths):
    spatial_out = spatial_block(motion, s_gain, s_query, s_key_value, s_out)
    frames, joints, width = motion.shape
    normed = layer_norm(spatial_out, t_gain).reshape(frames * joints, width)
    queries = jnp.dot(normed, t_query, preferred_element_type=jnp.float32).astype(jnp.bfloat16)
    queries = queries.reshape(frames, joints, HEADS, HEAD)
    pairs = jnp.dot(normed, t_key_value.reshape(width, 2 * width), preferred_element_type=jnp.float32).astype(jnp.bfloat16)
    pairs = pairs.reshape(frames, joints, 2, HEADS, HEAD)
    frame_ids = jnp.arange(frames, dtype=jnp.int32)
    clips = clip_index(frame_ids, lengths)
    allowed = (frame_ids[None, :] <= frame_ids[:, None]) & (clips[None, :] == clips[:, None])
    scale = 1.0 / jnp.sqrt(jnp.float32(HEAD))

    def one_joint(items):
        query_rows, key_rows, value_rows = items
        scores = jnp.einsum('fhe,ghe->hfg', query_rows, key_rows, preferred_element_type=jnp.float32) * scale
        masked = jnp.where(allowed[None], scores, jnp.float32(-1e+30))
        peak = lax.optimization_barrier(jnp.max(masked, axis=-1, keepdims=True))
        weights = jnp.where(allowed[None], jnp.exp(masked - peak), jnp.float32(0.0))
        total = lax.optimization_barrier(jnp.sum(weights, axis=-1))
        mixed = jnp.einsum('hfg,ghe->fhe', weights.astype(jnp.bfloat16), value_rows, preferred_element_type=jnp.float32)
        return (mixed / jnp.transpose(total)[..., None]).astype(jnp.bfloat16)
    context = lax.map(one_joint, (jnp.transpose(queries, (1, 0, 2, 3)), jnp.transpose(pairs[:, :, 0], (1, 0, 2, 3)), jnp.transpose(pairs[:, :, 1], (1, 0, 2, 3))))
    context = jnp.transpose(context, (1, 0, 2, 3)).reshape(frames * joints, width)
    temporal_branch = jnp.dot(context, t_out, preferred_element_type=jnp.float32).astype(jnp.bfloat16).reshape(frames, joints, width)
    return (spatial_out, temporal_branch)
```

```python
import functools

import jax
import jax.numpy as jnp
from jax import lax
from jax.experimental import pallas as pl
from jax.experimental.pallas import tpu as pltpu
from jax.sharding import PartitionSpec as P

HEAD = 64
TILE = 256
GROUP = TILE // HEAD
MESH = pl.DeviceIdType.MESH
F32 = jnp.float32
BF16 = jnp.bfloat16


def layer_norm(wide, gain):
    mean = jnp.mean(wide, axis=-1, keepdims=True)
    centred = wide - mean
    spread = jnp.mean(centred * centred, axis=-1, keepdims=True)
    return (centred * lax.rsqrt(spread + 1e-05) * gain).astype(BF16)


def dot(a, b):
    return jnp.dot(a, b, preferred_element_type=F32)


def kernel(
    n, cols, clips,
    len_ref, x_ref, sg_ref, tg_ref, sq_hbm, skv_hbm, so_hbm, tq_hbm, tkv_hbm, to_hbm,
    sp_ref, out_ref,
    sq, skv, so, tq, tkv, to, a_ref, ctx_ref, nb_ref, blk, qm, m_ref, l_ref, acc_ref,
    lsem, wsend, wrecv, hsend, hrecv, zsend, ysend, recv,
):
    joints, half, width = x_ref.shape
    span = 2 * half
    rows = joints * half
    window = n // 2
    tiles = width // TILE
    per_half = tiles // 2
    me = lax.axis_index("seq")
    core = lax.axis_index("joint")
    other = {"joint": 1 - core}

    local = [
        pltpu.make_async_copy(src, dst, lsem.at[k])
        for k, (src, dst) in enumerate(
            [(sq_hbm, sq), (skv_hbm, skv), (so_hbm, so),
             (tq_hbm, tq.at[0]), (tkv_hbm, tkv.at[0]), (to_hbm, to.at[0])]
        )
    ]
    for copy in local:
        copy.start()

    if cols == 2:
        y = lax.rem(me, 2)
        mate = me + 1 - 2 * y
        partners = [(None, other), (None, {"seq": mate}),
                    (me + 2 < n, {"seq": me + 2}), (me >= 2, {"seq": me - 2})]
    else:
        partners = [(None, other), (me + 1 < n, {"seq": me + 1}), (me >= 1, {"seq": me - 1})]
    barrier = pltpu.get_barrier_semaphore()

    def guarded(cond, action):
        if cond is None:
            action()
        else:
            pl.when(cond)(action)

    for cond, where in partners:
        guarded(cond, lambda where=where: pl.semaphore_signal(
            barrier, inc=1, device_id=where, device_id_type=MESH))
    peers = sum(1 if cond is None else jnp.where(cond, 1, 0) for cond, where in partners)
    pl.semaphore_wait(barrier, peers)

    weights = [
        pltpu.make_async_remote_copy(
            src_ref=src, dst_ref=dst.at[1], send_sem=wsend.at[k], recv_sem=wrecv.at[k],
            device_id=other, device_id_type=MESH)
        for k, (src, dst) in enumerate([(tq_hbm, tq), (tkv_hbm, tkv), (to_hbm, to)])
    ]
    for copy in weights:
        copy.start()

    x = x_ref[...].reshape(rows, width).astype(F32)
    a_ref[...] = layer_norm(x, sg_ref[...])
    er = lax.broadcasted_iota(jnp.int32, (TILE, TILE), 0) >> 6
    ec = lax.broadcasted_iota(jnp.int32, (TILE, TILE), 1) >> 6
    ones = jnp.where(er == ec, 1.0, 0.0).astype(BF16)
    local[0].wait()
    local[1].wait()

    def spatial_tile(t, carry):
        c0 = pl.multiple_of(t * TILE, TILE)
        a = a_ref[...]
        q = dot(a, sq[:, pl.ds(c0, TILE)]).astype(BF16).astype(F32)
        k = dot(a, skv[:, pl.ds(c0, TILE)]).astype(BF16).astype(F32)
        v = dot(a, skv[:, pl.ds(pl.multiple_of(width + t * TILE, TILE), TILE)]).astype(BF16).astype(F32)
        prods = jnp.concatenate(
            [q[j * half:(j + 1) * half] * k[i * half:(i + 1) * half]
             for j in range(2) for i in range(2)], axis=0)
        hi = prods.astype(BF16)
        lo = (prods - hi.astype(F32)).astype(BF16)
        s = (dot(hi, ones) + dot(lo, ones)) * 0.125
        for j in range(2):
            s0 = s[(2 * j) * half:(2 * j + 1) * half]
            s1 = s[(2 * j + 1) * half:(2 * j + 2) * half]
            m = jnp.maximum(s0, s1)
            p0 = jnp.exp(s0 - m)
            p1 = jnp.exp(s1 - m)
            total = p0 + p1
            mixed = (p0.astype(BF16).astype(F32) * v[:half] + p1.astype(BF16).astype(F32) * v[half:])
            ctx_ref[pl.ds(j * half, half), pl.ds(c0, TILE)] = (mixed / total).astype(BF16)
        return carry

    lax.fori_loop(0, tiles, spatial_tile, 0)
    local[2].wait()

    def spatial_out(t, carry):
        c0 = pl.multiple_of(t * TILE, TILE)
        update = dot(ctx_ref[...], so[:, pl.ds(c0, TILE)])
        res = x_ref[:, :, pl.ds(c0, TILE)].astype(F32) + update.reshape(joints, half, TILE)
        sp_ref[:, :, pl.ds(c0, TILE)] = res.astype(BF16)
        return carry

    lax.fori_loop(0, tiles, spatial_out, 0)
    nb_ref[...] = layer_norm(
        sp_ref[...].reshape(rows, width).astype(F32), tg_ref[...]).reshape(joints, half, width)

    mine = pl.ds(pl.multiple_of(core * half, half), half)
    swap = pltpu.make_async_remote_copy(
        src_ref=nb_ref.at[1 - core], dst_ref=blk.at[0, mine, :],
        send_sem=hsend.at[0], recv_sem=hrecv.at[0], device_id=other, device_id_type=MESH)
    swap.start()
    blk[0, mine, :] = nb_ref[core]
    swap.wait_recv()

    sends = []

    def send(cond, src, dst, sem, target):
        copy = pltpu.make_async_remote_copy(
            src_ref=blk.at[src], dst_ref=blk.at[dst], send_sem=sem, recv_sem=recv.at[dst],
            device_id={"seq": target}, device_id_type=MESH)
        pl.when(cond)(copy.start)
        sends.append((cond, copy))

    def forward(slot):
        have = me >= slot
        if cols == 2:
            if slot % 2:
                return
            step = slot // 2
            if slot + 2 <= window:
                send(have & (me + 2 < n), slot, slot + 2, zsend.at[step], me + 2)
            if slot == 0:
                send(y == 0, 0, 1, ysend.at[0], mate)
            elif slot + 1 <= window:
                send(have, slot, slot + 1 - 2 * y, ysend.at[step], mate)
            else:
                send(have & (y == 1), slot, slot - 1, ysend.at[step], mate)
        elif slot + 1 <= window:
            send(have & (me + 1 < n), slot, slot + 1, zsend.at[slot], me + 1)

    forward(0)

    for copy in local[3:]:
        copy.wait()
    for copy in weights:
        copy.wait_recv()
    lane = lax.broadcasted_iota(jnp.int32, (1, TILE), 1) >> 6
    pick = [lane == g for g in range(GROUP)]

    def query_tile(t, carry):
        c0 = pl.multiple_of(lax.rem(t, per_half) * TILE, TILE)
        q = dot(blk[0], tq[t // per_half, :, pl.ds(c0, TILE)]).astype(BF16).astype(F32) * 0.125
        for g in range(GROUP):
            qm[t, pl.ds(g * span, span), :] = jnp.where(pick[g], q, 0.0).astype(BF16)
        return carry

    lax.fori_loop(0, tiles, query_tile, 0)

    query = lax.broadcasted_iota(jnp.int32, (span, span), 0) + me * span
    first = jnp.zeros((span, span), jnp.int32)
    end = jnp.int32(0)
    for c in range(clips):
        end = end + len_ref[c]
        first = jnp.where(query >= end, end, first)
    column = lax.broadcasted_iota(jnp.int32, (span, span), 1)

    def by_head(parts):
        res = parts[GROUP - 1]
        for g in range(GROUP - 2, -1, -1):
            res = jnp.where(pick[g], parts[g], res)
        return res

    def attend(slot):
        key = column + (me - slot) * span
        seen = key >= first
        if slot == 0:
            seen = seen & (key <= query)
        bias = jnp.where(seen, 0.0, -1e30).astype(F32)
        bias = jnp.concatenate([bias] * GROUP, axis=0)

        def tile(t, carry):
            b = blk[slot]
            h = t // per_half
            c0 = lax.rem(t, per_half) * TILE
            k = dot(b, tkv[h, :, pl.ds(pl.multiple_of(c0, TILE), TILE)]).astype(BF16)
            v = dot(b, tkv[h, :, pl.ds(pl.multiple_of(width // 2 + c0, TILE), TILE)]).astype(BF16)
            s = lax.dot_general(qm[t], k, (((1,), (1,)), ((), ())), preferred_element_type=F32)
            s = s + bias
            top = jnp.max(s, axis=-1, keepdims=True)
            if slot == 0:
                m = jnp.broadcast_to(top, s.shape)
                p = jnp.exp(s - m)
                l_ref[t] = p
            else:
                old = m_ref[t]
                m = jnp.maximum(old, top)
                p = jnp.exp(s - m)
                fade = jnp.exp(old - m)
                l_ref[t] = l_ref[t] * fade + p
            m_ref[t] = m
            pv = dot(p.astype(BF16), v)
            new = by_head([pv[g * span:(g + 1) * span] for g in range(GROUP)])
            if slot == 0:
                acc_ref[t] = new
            else:
                keep = by_head([jnp.concatenate([fade[g * span:(g + 1) * span]] * 2, axis=1)
                                for g in range(GROUP)])
                acc_ref[t] = acc_ref[t] * keep + new
            return carry

        lax.fori_loop(0, tiles, tile, 0)

    attend(0)

    if cols == 2:
        order = [s for m in range(2, window + 1, 2) for s in (m, m - 1)]
    else:
        order = list(range(1, window + 1))
    for slot in order:
        @pl.when(me >= slot)
        def _(slot=slot):
            pltpu.make_async_copy(blk.at[slot], blk.at[slot], recv.at[slot]).wait()
        forward(slot)

        @pl.when(me >= slot)
        def _(slot=slot):
            attend(slot)

    def finish(t, carry):
        c0 = pl.multiple_of(t * TILE, TILE)
        total = jnp.sum(l_ref[t], axis=-1, keepdims=True)
        parts = [jnp.broadcast_to(total[g * span:(g + 1) * span], (span, TILE)) for g in range(GROUP)]
        ctx_ref[:, pl.ds(c0, TILE)] = (acc_ref[t] / by_head(parts)).astype(BF16)
        return carry

    lax.fori_loop(0, tiles, finish, 0)

    def project(t, carry):
        c0 = pl.multiple_of(t * TILE, TILE)
        hw = width // 2
        res = dot(ctx_ref[:, :hw], to[0, :, pl.ds(c0, TILE)]) + dot(ctx_ref[:, hw:], to[1, :, pl.ds(c0, TILE)])
        out_ref[:, pl.ds(c0, TILE)] = res.astype(BF16)
        return carry

    lax.fori_loop(0, tiles, project, 0)

    for cond, copy in sends:
        pl.when(cond)(copy.wait_send)
    swap.wait_send()
    for copy in weights:
        copy.wait_send()


def shards(n, cols, motion, s_gain, s_query, s_key_value, s_out, t_gain, t_query, t_key_value, t_out, lengths):
    half, joints, width = motion.shape
    span = 2 * half
    hw = width // 2
    window = n // 2
    tiles = width // TILE
    x = jnp.transpose(motion, (1, 0, 2))
    skv = s_key_value.reshape(width, 2 * width)
    tkv = t_key_value.reshape(width, 2 * hw)
    vmem = pl.BlockSpec(memory_space=pltpu.VMEM)
    hbm = pl.BlockSpec(memory_space=pl.ANY)
    sp, out = pl.pallas_call(
        functools.partial(kernel, n, cols, lengths.shape[0]),
        out_shape=(jax.ShapeDtypeStruct((joints, half, width), BF16),
                   jax.ShapeDtypeStruct((span, width), BF16)),
        in_specs=[pl.BlockSpec(memory_space=pltpu.SMEM), vmem, vmem, vmem] + [hbm] * 6,
        out_specs=(vmem, vmem),
        scratch_shapes=[
            pltpu.VMEM((width, width), BF16),
            pltpu.VMEM((width, 2 * width), BF16),
            pltpu.VMEM((width, width), BF16),
            pltpu.VMEM((2, width, hw), BF16),
            pltpu.VMEM((2, width, 2 * hw), BF16),
            pltpu.VMEM((2, hw, width), BF16),
            pltpu.VMEM((joints * half, width), BF16),
            pltpu.VMEM((span, width), BF16),
            pltpu.VMEM((joints, half, width), BF16),
            pltpu.VMEM((window + 1, span, width), BF16),
            pltpu.VMEM((tiles, GROUP * span, TILE), BF16),
            pltpu.VMEM((tiles, GROUP * span, span), F32),
            pltpu.VMEM((tiles, GROUP * span, span), F32),
            pltpu.VMEM((tiles, span, TILE), F32),
            pltpu.SemaphoreType.DMA((6,)),
            pltpu.SemaphoreType.DMA((3,)),
            pltpu.SemaphoreType.DMA((3,)),
            pltpu.SemaphoreType.DMA((1,)),
            pltpu.SemaphoreType.DMA((1,)),
            pltpu.SemaphoreType.DMA((window + 1,)),
            pltpu.SemaphoreType.DMA((window + 1,)),
            pltpu.SemaphoreType.DMA((window + 1,)),
        ],
        compiler_params=pltpu.CompilerParams(
            collective_id=0, has_side_effects=True, vmem_limit_bytes=48 * 1024 * 1024),
    )(lengths, x, s_gain.reshape(1, width), t_gain.reshape(1, width),
      s_query, skv, s_out, t_query, tkv, t_out)
    return jnp.transpose(sp, (1, 0, 2)), out.reshape(span, 1, width)


def solution(mesh):
    n = mesh.shape["seq"]
    cols = 2 if n == 8 else 1
    in_specs = (
        P(("parts", "seq", "joint"), None, None),
        P(),
        P(),
        P(),
        P(),
        P(),
        P(None, "joint"),
        P(None, None, "joint"),
        P("joint", None),
        P("parts"),
    )
    out_specs = (P(("parts", "seq", "joint"), None, None), P(("parts", "seq"), "joint", None))
    return jax.shard_map(
        functools.partial(shards, n, cols), mesh=mesh, in_specs=in_specs, out_specs=out_specs, check_vma=False)
```

```python
import functools

import jax
import jax.numpy as jnp
from jax import lax
from jax.experimental import pallas as pl
from jax.experimental.pallas import tpu as pltpu
from jax.sharding import PartitionSpec as P

HEAD = 64
TILE = 256
GROUP = TILE // HEAD
MESH = pl.DeviceIdType.MESH
F32 = jnp.float32
BF16 = jnp.bfloat16


def layer_norm(wide, gain):
    mean = jnp.mean(wide, axis=-1, keepdims=True)
    centred = wide - mean
    spread = jnp.mean(centred * centred, axis=-1, keepdims=True)
    return (centred * lax.rsqrt(spread + 1e-05) * gain).astype(BF16)


def dot(a, b):
    return jnp.dot(a, b, preferred_element_type=F32)


def kernel(
    n, cols, clips,
    len_ref, x_ref, sg_ref, tg_ref, sq, skv, so, tq, tkv, to,
    sp_ref, out_ref,
    otq, otkv, oto, a_ref, ctx_ref, nb_ref, blk, qm, m_ref, l_ref, acc_ref,
    wsend, wrecv, isend, zsend, ysend, recv,
):
    joints, half, width = x_ref.shape
    span = 2 * half
    rows = joints * half
    window = n // 2
    tiles = width // TILE
    per_half = tiles // 2
    me = lax.axis_index("seq")
    core = lax.axis_index("joint")
    other = {"joint": 1 - core}

    def both(where):
        return [{"seq": where, "joint": core}, {"seq": where, "joint": 1 - core}]

    hop = cols
    partners = [(None, other)]
    if cols == 2:
        y = lax.rem(me, 2)
        mate = me + 1 - 2 * y
        partners += [(None, dev) for dev in both(mate)]
    partners += [(me + hop < n, dev) for dev in both(me + hop)]
    partners += [(me >= hop, dev) for dev in both(me - hop)]
    barrier = pltpu.get_barrier_semaphore()

    def guarded(cond, action):
        if cond is None:
            action()
        else:
            pl.when(cond)(action)

    for cond, where in partners:
        guarded(cond, lambda where=where: pl.semaphore_signal(
            barrier, inc=1, device_id=where, device_id_type=MESH))
    peers = sum(1 if cond is None else jnp.where(cond, 1, 0) for cond, where in partners)

    x = x_ref[...].reshape(rows, width).astype(F32)
    a_ref[...] = layer_norm(x, sg_ref[...])

    pl.semaphore_wait(barrier, peers)
    weights = [
        pltpu.make_async_remote_copy(
            src_ref=src, dst_ref=dst, send_sem=wsend.at[k], recv_sem=wrecv.at[k],
            device_id=other, device_id_type=MESH)
        for k, (src, dst) in enumerate([(tq, otq), (tkv, otkv), (to, oto)])
    ]
    for copy in weights:
        copy.start()

    er = lax.broadcasted_iota(jnp.int32, (TILE, TILE), 0) >> 6
    ec = lax.broadcasted_iota(jnp.int32, (TILE, TILE), 1) >> 6
    ones = jnp.where(er == ec, 1.0, 0.0).astype(BF16)

    def spatial_tile(t, carry):
        c0 = pl.multiple_of(t * TILE, TILE)
        a = a_ref[...]
        q = dot(a, sq[:, pl.ds(c0, TILE)]).astype(BF16).astype(F32)
        k = dot(a, skv[:, pl.ds(c0, TILE)]).astype(BF16).astype(F32)
        v = dot(a, skv[:, pl.ds(pl.multiple_of(width + t * TILE, TILE), TILE)]).astype(BF16).astype(F32)
        prods = jnp.concatenate(
            [q[j * half:(j + 1) * half] * k[i * half:(i + 1) * half]
             for j in range(2) for i in range(2)], axis=0)
        hi = prods.astype(BF16)
        lo = (prods - hi.astype(F32)).astype(BF16)
        s = (dot(hi, ones) + dot(lo, ones)) * 0.125
        for j in range(2):
            s0 = s[(2 * j) * half:(2 * j + 1) * half]
            s1 = s[(2 * j + 1) * half:(2 * j + 2) * half]
            m = jnp.maximum(s0, s1)
            p0 = jnp.exp(s0 - m)
            p1 = jnp.exp(s1 - m)
            total = p0 + p1
            mixed = (p0.astype(BF16).astype(F32) * v[:half] + p1.astype(BF16).astype(F32) * v[half:])
            ctx_ref[pl.ds(j * half, half), pl.ds(c0, TILE)] = (mixed / total).astype(BF16)
        return carry

    lax.fori_loop(0, tiles, spatial_tile, 0)

    def spatial_out(t, carry):
        c0 = pl.multiple_of(t * TILE, TILE)
        update = dot(ctx_ref[...], so[:, pl.ds(c0, TILE)])
        res = x_ref[:, :, pl.ds(c0, TILE)].astype(F32) + update.reshape(joints, half, TILE)
        sp_ref[:, :, pl.ds(c0, TILE)] = res.astype(BF16)
        return carry

    lax.fori_loop(0, tiles, spatial_out, 0)
    nb_ref[...] = layer_norm(
        sp_ref[...].reshape(rows, width).astype(F32), tg_ref[...]).reshape(joints, half, width)

    mine = pl.ds(pl.multiple_of(core * half, half), half)
    sends = []

    def send(cond, src, slot, part, sem, where):
        at = pl.ds(pl.multiple_of(part * half, half), half)
        copy = pltpu.make_async_remote_copy(
            src_ref=src, dst_ref=blk.at[slot, at, :], send_sem=sem, recv_sem=recv.at[slot, part],
            device_id=where, device_id_type=MESH)
        guarded(cond, copy.start)
        sends.append((cond, copy))

    fits = me + hop < n
    ahead = both(me + hop)
    send(fits, nb_ref.at[core], hop, core, isend.at[0], ahead[0])
    send(fits, nb_ref.at[1 - core], hop, core, isend.at[1], ahead[1])
    send(None, nb_ref.at[1 - core], 0, core, isend.at[2], other)
    if cols == 2:
        beside = both(mate)
        send(y == 0, nb_ref.at[core], 1, core, isend.at[3], beside[0])
        send(y == 0, nb_ref.at[1 - core], 1, core, isend.at[4], beside[1])
    blk[0, mine, :] = nb_ref[core]

    def arrived(slot, part):
        view = blk.at[slot, pl.ds(pl.multiple_of(part * half, half), half), :]
        pltpu.make_async_copy(view, view, recv.at[slot, part]).wait()

    def forward(slot, part):
        have = me >= slot
        src = blk.at[slot, pl.ds(part * half, half), :]
        if slot % hop == 0 and slot + hop <= window:
            send(have & fits, src, slot + hop, part, zsend.at[slot, part], both(me + hop)[0])
        if cols == 2 and slot % 2 == 0:
            if slot + 1 <= window:
                send(have, src, slot + 1 - 2 * y, part, ysend.at[slot, part], both(mate)[0])
            else:
                send(have & (y == 1), src, slot - 1, part, ysend.at[slot, part], both(mate)[0])

    arrived(0, 1 - core)

    lane = lax.broadcasted_iota(jnp.int32, (1, TILE), 1) >> 6
    pick = [lane == g for g in range(GROUP)]
    wq, wkv = (tq, otq), (tkv, otkv)

    def queries(h):
        def query_tile(t, carry):
            c0 = pl.multiple_of(t * TILE, TILE)
            q = dot(blk[0], wq[h][:, pl.ds(c0, TILE)]).astype(BF16).astype(F32) * 0.125
            for g in range(GROUP):
                qm[h * per_half + t, pl.ds(g * span, span), :] = jnp.where(pick[g], q, 0.0).astype(BF16)
            return carry

        lax.fori_loop(0, per_half, query_tile, 0)

    query = lax.broadcasted_iota(jnp.int32, (span, span), 0) + me * span
    first = jnp.zeros((span, span), jnp.int32)
    end = jnp.int32(0)
    for c in range(clips):
        end = end + len_ref[c]
        first = jnp.where(query >= end, end, first)
    column = lax.broadcasted_iota(jnp.int32, (span, span), 1)

    def by_head(parts):
        res = parts[GROUP - 1]
        for g in range(GROUP - 2, -1, -1):
            res = jnp.where(pick[g], parts[g], res)
        return res

    def attend(slot, h):
        key = column + (me - slot) * span
        seen = key >= first
        if slot == 0:
            seen = seen & (key <= query)
        bias = jnp.where(seen, 0.0, -1e30).astype(F32)
        bias = jnp.concatenate([bias] * GROUP, axis=0)

        def tile(u, carry):
            t = h * per_half + u
            b = blk[slot]
            c0 = u * TILE
            k = dot(b, wkv[h][:, pl.ds(pl.multiple_of(c0, TILE), TILE)]).astype(BF16)
            v = dot(b, wkv[h][:, pl.ds(pl.multiple_of(width // 2 + c0, TILE), TILE)]).astype(BF16)
            s = lax.dot_general(qm[t], k, (((1,), (1,)), ((), ())), preferred_element_type=F32)
            s = s + bias
            top = jnp.max(s, axis=-1, keepdims=True)
            if slot == 0:
                m = jnp.broadcast_to(top, s.shape)
                p = jnp.exp(s - m)
                l_ref[t] = p
            else:
                old = m_ref[t]
                m = jnp.maximum(old, top)
                p = jnp.exp(s - m)
                fade = jnp.exp(old - m)
                l_ref[t] = l_ref[t] * fade + p
            m_ref[t] = m
            pv = dot(p.astype(BF16), v)
            new = by_head([pv[g * span:(g + 1) * span] for g in range(GROUP)])
            if slot == 0:
                acc_ref[t] = new
            else:
                keep = by_head([jnp.concatenate([fade[g * span:(g + 1) * span]] * 2, axis=1)
                                for g in range(GROUP)])
                acc_ref[t] = acc_ref[t] * keep + new
            return carry

        lax.fori_loop(0, per_half, tile, 0)

    queries(0)
    attend(0, 0)
    weights[0].wait_recv()
    queries(1)
    weights[1].wait_recv()
    attend(0, 1)

    if cols == 2:
        order = [s for m in range(2, window + 1, 2) for s in (m, m - 1)]
    else:
        order = list(range(1, window + 1))
    for slot in order:
        for part in range(2):
            pl.when(me >= slot)(lambda slot=slot, part=part: arrived(slot, part))
            forward(slot, part)

        @pl.when(me >= slot)
        def _(slot=slot):
            attend(slot, 0)
            attend(slot, 1)

    def finish(t, carry):
        c0 = pl.multiple_of(t * TILE, TILE)
        total = jnp.sum(l_ref[t], axis=-1, keepdims=True)
        parts = [jnp.broadcast_to(total[g * span:(g + 1) * span], (span, TILE)) for g in range(GROUP)]
        ctx_ref[:, pl.ds(c0, TILE)] = (acc_ref[t] / by_head(parts)).astype(BF16)
        return carry

    lax.fori_loop(0, tiles, finish, 0)
    weights[2].wait_recv()

    def project(t, carry):
        c0 = pl.multiple_of(t * TILE, TILE)
        hw = width // 2
        res = dot(ctx_ref[:, :hw], to[:, pl.ds(c0, TILE)]) + dot(ctx_ref[:, hw:], oto[:, pl.ds(c0, TILE)])
        out_ref[:, pl.ds(c0, TILE)] = res.astype(BF16)
        return carry

    lax.fori_loop(0, tiles, project, 0)

    for cond, copy in sends:
        guarded(cond, copy.wait_send)
    for copy in weights:
        copy.wait_send()


def shards(n, cols, motion, s_gain, s_query, s_key_value, s_out, t_gain, t_query, t_key_value, t_out, lengths):
    half, joints, width = motion.shape
    span = 2 * half
    hw = width // 2
    window = n // 2
    tiles = width // TILE
    x = jnp.transpose(motion, (1, 0, 2))
    skv = s_key_value.reshape(width, 2 * width)
    tkv = t_key_value.reshape(width, 2 * hw)
    vmem = pl.BlockSpec(memory_space=pltpu.VMEM)
    sp, out = pl.pallas_call(
        functools.partial(kernel, n, cols, lengths.shape[0]),
        out_shape=(jax.ShapeDtypeStruct((joints, half, width), BF16),
                   jax.ShapeDtypeStruct((span, width), BF16)),
        in_specs=[pl.BlockSpec(memory_space=pltpu.SMEM), vmem, vmem, vmem] + [vmem] * 6,
        out_specs=(vmem, vmem),
        scratch_shapes=[
            pltpu.VMEM((width, hw), BF16),
            pltpu.VMEM((width, 2 * hw), BF16),
            pltpu.VMEM((hw, width), BF16),
            pltpu.VMEM((joints * half, width), BF16),
            pltpu.VMEM((span, width), BF16),
            pltpu.VMEM((joints, half, width), BF16),
            pltpu.VMEM((window + 1, span, width), BF16),
            pltpu.VMEM((tiles, GROUP * span, TILE), BF16),
            pltpu.VMEM((tiles, GROUP * span, span), F32),
            pltpu.VMEM((tiles, GROUP * span, span), F32),
            pltpu.VMEM((tiles, span, TILE), F32),
            pltpu.SemaphoreType.DMA((3,)),
            pltpu.SemaphoreType.DMA((3,)),
            pltpu.SemaphoreType.DMA((5,)),
            pltpu.SemaphoreType.DMA((window + 1, 2)),
            pltpu.SemaphoreType.DMA((window + 1, 2)),
            pltpu.SemaphoreType.DMA((window + 1, 2)),
        ],
        compiler_params=pltpu.CompilerParams(
            collective_id=0, has_side_effects=True, vmem_limit_bytes=36 * 1024 * 1024),
    )(lengths, x, s_gain.reshape(1, width), t_gain.reshape(1, width),
      s_query, skv, s_out, t_query, tkv, t_out)
    return jnp.transpose(sp, (1, 0, 2)), out.reshape(span, 1, width)


def solution(mesh):
    n = mesh.shape["seq"]
    cols = 2 if n == 8 else 1
    in_specs = (
        P(("parts", "seq", "joint"), None, None),
        P(),
        P(),
        P(),
        P(),
        P(),
        P(None, "joint"),
        P(None, None, "joint"),
        P("joint", None),
        P("parts"),
    )
    out_specs = (P(("parts", "seq", "joint"), None, None), P(("parts", "seq"), "joint", None))
    return jax.shard_map(
        functools.partial(shards, n, cols), mesh=mesh, in_specs=in_specs, out_specs=out_specs, check_vma=False)
```

```python
import functools

import jax
import jax.numpy as jnp
from jax import lax
from jax.experimental import pallas as pl
from jax.experimental.pallas import tpu as pltpu
from jax.sharding import PartitionSpec as P

HEAD = 64
TILE = 256
GROUP = TILE // HEAD
MESH = pl.DeviceIdType.MESH
F32 = jnp.float32
BF16 = jnp.bfloat16


def layer_norm(wide, gain):
    mean = jnp.mean(wide, axis=-1, keepdims=True)
    centred = wide - mean
    spread = jnp.mean(centred * centred, axis=-1, keepdims=True)
    return (centred * lax.rsqrt(spread + 1e-05) * gain).astype(BF16)


def dot(a, b):
    return jnp.dot(a, b, preferred_element_type=F32)


def kernel(
    n, cols, clips,
    len_ref, x_ref, sg_ref, tg_ref, sq, skv, so, tq, tkv, to,
    sp_ref, out_ref,
    otq, otkv, oto, a_ref, ctx_ref, nb_ref, blk, qm, m_ref, l_ref, acc_ref,
    wsend, wrecv, isend, zsend, ysend, recv,
):
    joints, half, width = x_ref.shape
    span = 2 * half
    rows = joints * half
    window = n // 2
    tiles = width // TILE
    per_half = tiles // 2
    me = lax.axis_index("seq")
    core = lax.axis_index("joint")
    other = {"joint": 1 - core}

    def both(where):
        return [{"seq": where, "joint": core}, {"seq": where, "joint": 1 - core}]

    hop = cols
    partners = [(None, other)]
    if cols == 2:
        y = lax.rem(me, 2)
        mate = me + 1 - 2 * y
        partners += [(None, dev) for dev in both(mate)]
    partners += [(me + hop < n, dev) for dev in both(me + hop)]
    partners += [(me >= hop, dev) for dev in both(me - hop)]
    barrier = pltpu.get_barrier_semaphore()

    def guarded(cond, action):
        if cond is None:
            action()
        else:
            pl.when(cond)(action)

    for cond, where in partners:
        guarded(cond, lambda where=where: pl.semaphore_signal(
            barrier, inc=1, device_id=where, device_id_type=MESH))
    peers = sum(1 if cond is None else jnp.where(cond, 1, 0) for cond, where in partners)

    x = x_ref[...].reshape(rows, width).astype(F32)
    a_ref[...] = layer_norm(x, sg_ref[...])

    pl.semaphore_wait(barrier, peers)
    weights = [
        pltpu.make_async_remote_copy(
            src_ref=src, dst_ref=dst, send_sem=wsend.at[k], recv_sem=wrecv.at[k],
            device_id=other, device_id_type=MESH)
        for k, (src, dst) in enumerate([(tq, otq), (tkv, otkv), (to, oto)])
    ]
    for copy in weights:
        copy.start()

    er = lax.broadcasted_iota(jnp.int32, (TILE, TILE), 0) >> 6
    ec = lax.broadcasted_iota(jnp.int32, (TILE, TILE), 1) >> 6
    ones = jnp.where(er == ec, 1.0, 0.0).astype(BF16)

    def spatial_tile(t, carry):
        c0 = pl.multiple_of(t * TILE, TILE)
        a = a_ref[...]
        q = dot(a, sq[:, pl.ds(c0, TILE)]).astype(BF16).astype(F32)
        k = dot(a, skv[:, pl.ds(c0, TILE)]).astype(BF16).astype(F32)
        v = dot(a, skv[:, pl.ds(pl.multiple_of(width + t * TILE, TILE), TILE)]).astype(BF16).astype(F32)
        prods = jnp.concatenate(
            [q[j * half:(j + 1) * half] * k[i * half:(i + 1) * half]
             for j in range(2) for i in range(2)], axis=0)
        hi = prods.astype(BF16)
        lo = (prods - hi.astype(F32)).astype(BF16)
        s = (dot(hi, ones) + dot(lo, ones)) * 0.125
        for j in range(2):
            s0 = s[(2 * j) * half:(2 * j + 1) * half]
            s1 = s[(2 * j + 1) * half:(2 * j + 2) * half]
            m = jnp.maximum(s0, s1)
            p0 = jnp.exp(s0 - m)
            p1 = jnp.exp(s1 - m)
            total = p0 + p1
            mixed = (p0.astype(BF16).astype(F32) * v[:half] + p1.astype(BF16).astype(F32) * v[half:])
            ctx_ref[pl.ds(j * half, half), pl.ds(c0, TILE)] = (mixed / total).astype(BF16)
        return carry

    lax.fori_loop(0, tiles, spatial_tile, 0)

    def spatial_out(t, carry):
        c0 = pl.multiple_of(t * TILE, TILE)
        update = dot(ctx_ref[...], so[:, pl.ds(c0, TILE)])
        res = x_ref[:, :, pl.ds(c0, TILE)].astype(F32) + update.reshape(joints, half, TILE)
        sp_ref[:, :, pl.ds(c0, TILE)] = res.astype(BF16)
        return carry

    lax.fori_loop(0, tiles, spatial_out, 0)
    nb_ref[...] = layer_norm(
        sp_ref[...].reshape(rows, width).astype(F32), tg_ref[...]).reshape(joints, half, width)

    mine = pl.ds(pl.multiple_of(core * half, half), half)
    sends = []

    def send(cond, src, slot, part, sem, where):
        at = pl.ds(pl.multiple_of(part * half, half), half)
        copy = pltpu.make_async_remote_copy(
            src_ref=src, dst_ref=blk.at[slot, at, :], send_sem=sem, recv_sem=recv.at[slot, part],
            device_id=where, device_id_type=MESH)
        guarded(cond, copy.start)
        sends.append((cond, copy))

    fits = me + hop < n
    ahead = both(me + hop)
    send(fits, nb_ref.at[core], hop, core, isend.at[0], ahead[0])
    send(fits, nb_ref.at[1 - core], hop, core, isend.at[1], ahead[1])
    send(None, nb_ref.at[1 - core], 0, core, isend.at[2], other)
    if cols == 2:
        beside = both(mate)
        send(y == 0, nb_ref.at[core], 1, core, isend.at[3], beside[0])
        send(y == 0, nb_ref.at[1 - core], 1, core, isend.at[4], beside[1])
    blk[0, mine, :] = nb_ref[core]

    def arrived(slot, part):
        view = blk.at[slot, pl.ds(pl.multiple_of(part * half, half), half), :]
        pltpu.make_async_copy(view, view, recv.at[slot, part]).wait()

    def forward(slot, part):
        have = me >= slot
        src = blk.at[slot, pl.ds(part * half, half), :]
        if slot % hop == 0 and slot + hop <= window:
            send(have & fits, src, slot + hop, part, zsend.at[slot, part], both(me + hop)[0])
        if cols == 2 and slot % 2 == 0:
            if slot + 1 <= window:
                send(have, src, slot + 1 - 2 * y, part, ysend.at[slot, part], both(mate)[0])
            elif part == 0:
                send(have & (y == 1), src, slot - 1, part, ysend.at[slot, part], both(mate)[0])
        if cols == 2 and slot == window - 3 and part == 1:
            send(have & fits & (y == 0), src, slot + 2, part, zsend.at[slot, part], both(me + hop)[0])

    arrived(0, 1 - core)

    lane = lax.broadcasted_iota(jnp.int32, (1, TILE), 1) >> 6
    pick = [lane == g for g in range(GROUP)]
    wq, wkv = (tq, otq), (tkv, otkv)

    def queries(h):
        def query_tile(t, carry):
            c0 = pl.multiple_of(t * TILE, TILE)
            q = dot(blk[0], wq[h][:, pl.ds(c0, TILE)]).astype(BF16).astype(F32) * 0.125
            for g in range(GROUP):
                qm[h * per_half + t, pl.ds(g * span, span), :] = jnp.where(pick[g], q, 0.0).astype(BF16)
            return carry

        lax.fori_loop(0, per_half, query_tile, 0)

    query = lax.broadcasted_iota(jnp.int32, (span, span), 0) + me * span
    first = jnp.zeros((span, span), jnp.int32)
    end = jnp.int32(0)
    for c in range(clips):
        end = end + len_ref[c]
        first = jnp.where(query >= end, end, first)
    column = lax.broadcasted_iota(jnp.int32, (span, span), 1)

    def by_head(parts):
        res = parts[GROUP - 1]
        for g in range(GROUP - 2, -1, -1):
            res = jnp.where(pick[g], parts[g], res)
        return res

    def attend(slots, h):
        start = slots[0] == 0
        count = len(slots)

        def shade(slot):
            key = column + (me - slot) * span
            seen = key >= first
            if slot == 0:
                seen = seen & (key <= query)
            return jnp.where(seen, 0.0, -1e30).astype(F32)

        bias = jnp.concatenate([shade(slot) for slot in slots], axis=1)
        bias = jnp.concatenate([bias] * GROUP, axis=0)

        def wide(col):
            return jnp.concatenate([col] * count, axis=1)

        def tile(u, carry):
            t = h * per_half + u
            b = jnp.concatenate([blk[slot] for slot in slots], axis=0)
            c0 = u * TILE
            k = dot(b, wkv[h][:, pl.ds(pl.multiple_of(c0, TILE), TILE)]).astype(BF16)
            v = dot(b, wkv[h][:, pl.ds(pl.multiple_of(width // 2 + c0, TILE), TILE)]).astype(BF16)
            s = lax.dot_general(qm[t], k, (((1,), (1,)), ((), ())), preferred_element_type=F32)
            s = s + bias
            top = jnp.max(s, axis=-1, keepdims=True)
            if start:
                m = jnp.broadcast_to(top, (GROUP * span, span))
            else:
                old = m_ref[t]
                m = jnp.maximum(old, top)
                fade = jnp.exp(old - m)
            p = jnp.exp(s - wide(m))
            total = sum(p[:, z * span:(z + 1) * span] for z in range(count))
            l_ref[t] = total if start else l_ref[t] * fade + total
            m_ref[t] = m
            pv = dot(p.astype(BF16), v)
            new = by_head([pv[g * span:(g + 1) * span] for g in range(GROUP)])
            if start:
                acc_ref[t] = new
            else:
                keep = by_head([jnp.concatenate([fade[g * span:(g + 1) * span]] * 2, axis=1)
                                for g in range(GROUP)])
                acc_ref[t] = acc_ref[t] * keep + new
            return carry

        lax.fori_loop(0, per_half, tile, 0)

    queries(0)
    attend([0], 0)
    weights[0].wait_recv()
    queries(1)
    weights[1].wait_recv()
    attend([0], 1)

    def take(slot):
        for part in range(2):
            pl.when(me >= slot)(lambda part=part: arrived(slot, part))
            forward(slot, part)

    def use(cond, slots):
        @pl.when(cond)
        def _():
            attend(slots, 0)
            attend(slots, 1)

    if cols == 2 and window == 4:
        take(2)
        use(me >= 2, [2])
        take(1)
        take(4)
        use(me >= 4, [1, 4])
        use((me >= 1) & (me < 4), [1])
        take(3)
        use(me >= 3, [3])
    else:
        for slot in range(1, window + 1):
            take(slot)
            use(me >= slot, [slot])

    def finish(t, carry):
        c0 = pl.multiple_of(t * TILE, TILE)
        total = jnp.sum(l_ref[t], axis=-1, keepdims=True)
        parts = [jnp.broadcast_to(total[g * span:(g + 1) * span], (span, TILE)) for g in range(GROUP)]
        ctx_ref[:, pl.ds(c0, TILE)] = (acc_ref[t] / by_head(parts)).astype(BF16)
        return carry

    lax.fori_loop(0, tiles, finish, 0)
    weights[2].wait_recv()

    def project(t, carry):
        c0 = pl.multiple_of(t * TILE, TILE)
        hw = width // 2
        res = dot(ctx_ref[:, :hw], to[:, pl.ds(c0, TILE)]) + dot(ctx_ref[:, hw:], oto[:, pl.ds(c0, TILE)])
        out_ref[:, pl.ds(c0, TILE)] = res.astype(BF16)
        return carry

    lax.fori_loop(0, tiles, project, 0)

    for cond, copy in sends:
        guarded(cond, copy.wait_send)
    for copy in weights:
        copy.wait_send()


def shards(n, cols, motion, s_gain, s_query, s_key_value, s_out, t_gain, t_query, t_key_value, t_out, lengths):
    half, joints, width = motion.shape
    span = 2 * half
    hw = width // 2
    window = n // 2
    tiles = width // TILE
    x = jnp.transpose(motion, (1, 0, 2))
    skv = s_key_value.reshape(width, 2 * width)
    tkv = t_key_value.reshape(width, 2 * hw)
    vmem = pl.BlockSpec(memory_space=pltpu.VMEM)
    sp, out = pl.pallas_call(
        functools.partial(kernel, n, cols, lengths.shape[0]),
        out_shape=(jax.ShapeDtypeStruct((joints, half, width), BF16),
                   jax.ShapeDtypeStruct((span, width), BF16)),
        in_specs=[pl.BlockSpec(memory_space=pltpu.SMEM), vmem, vmem, vmem] + [vmem] * 6,
        out_specs=(vmem, vmem),
        scratch_shapes=[
            pltpu.VMEM((width, hw), BF16),
            pltpu.VMEM((width, 2 * hw), BF16),
            pltpu.VMEM((hw, width), BF16),
            pltpu.VMEM((joints * half, width), BF16),
            pltpu.VMEM((span, width), BF16),
            pltpu.VMEM((joints, half, width), BF16),
            pltpu.VMEM((window + 1, span, width), BF16),
            pltpu.VMEM((tiles, GROUP * span, TILE), BF16),
            pltpu.VMEM((tiles, GROUP * span, span), F32),
            pltpu.VMEM((tiles, GROUP * span, span), F32),
            pltpu.VMEM((tiles, span, TILE), F32),
            pltpu.SemaphoreType.DMA((3,)),
            pltpu.SemaphoreType.DMA((3,)),
            pltpu.SemaphoreType.DMA((5,)),
            pltpu.SemaphoreType.DMA((window + 1, 2)),
            pltpu.SemaphoreType.DMA((window + 1, 2)),
            pltpu.SemaphoreType.DMA((window + 1, 2)),
        ],
        compiler_params=pltpu.CompilerParams(
            collective_id=0, has_side_effects=True, vmem_limit_bytes=36 * 1024 * 1024),
    )(lengths, x, s_gain.reshape(1, width), t_gain.reshape(1, width),
      s_query, skv, s_out, t_query, tkv, t_out)
    return jnp.transpose(sp, (1, 0, 2)), out.reshape(span, 1, width)


def solution(mesh):
    n = mesh.shape["seq"]
    cols = 2 if n == 8 else 1
    in_specs = (
        P(("parts", "seq", "joint"), None, None),
        P(),
        P(),
        P(),
        P(),
        P(),
        P(None, "joint"),
        P(None, None, "joint"),
        P("joint", None),
        P("parts"),
    )
    out_specs = (P(("parts", "seq", "joint"), None, None), P(("parts", "seq"), "joint", None))
    return jax.shard_map(
        functools.partial(shards, n, cols), mesh=mesh, in_specs=in_specs, out_specs=out_specs, check_vma=False)
```

```python
import functools

import jax
import jax.numpy as jnp
from jax import lax
from jax.experimental import pallas as pl
from jax.experimental.pallas import tpu as pltpu
from jax.sharding import PartitionSpec as P

HEAD = 64
TILE = 256
GROUP = TILE // HEAD
MESH = pl.DeviceIdType.MESH
F32 = jnp.float32
BF16 = jnp.bfloat16


def layer_norm(wide, gain):
    mean = jnp.mean(wide, axis=-1, keepdims=True)
    centred = wide - mean
    spread = jnp.mean(centred * centred, axis=-1, keepdims=True)
    return (centred * lax.rsqrt(spread + 1e-05) * gain).astype(BF16)


def dot(a, b):
    return jnp.dot(a, b, preferred_element_type=F32)


def kernel(
    n, cols, clips,
    len_ref, x_ref, sg_ref, tg_ref, sq, skv, so, tq, tkv, to,
    sp_ref, out_ref,
    otq, otkv, oto, a_ref, ctx_ref, nb_ref, blk, qm, m_ref, l_ref, acc_ref,
    wsend, wrecv, isend, zsend, ysend, recv,
):
    joints, half, width = x_ref.shape
    span = 2 * half
    rows = joints * half
    window = n // 2
    tiles = width // TILE
    per_half = tiles // 2
    me = lax.axis_index("seq")
    core = lax.axis_index("joint")
    other = {"joint": 1 - core}

    def both(where):
        return [{"seq": where, "joint": core}, {"seq": where, "joint": 1 - core}]

    hop = cols
    both_tiles = per_half if cols == 2 else 1
    partners = [(None, other)]
    if cols == 2:
        y = lax.rem(me, 2)
        mate = me + 1 - 2 * y
        partners += [(None, dev) for dev in both(mate)]
    partners += [(me + hop < n, dev) for dev in both(me + hop)]
    partners += [(me >= hop, dev) for dev in both(me - hop)]
    barrier = pltpu.get_barrier_semaphore()

    def guarded(cond, action):
        if cond is None:
            action()
        else:
            pl.when(cond)(action)

    for cond, where in partners:
        guarded(cond, lambda where=where: pl.semaphore_signal(
            barrier, inc=1, device_id=where, device_id_type=MESH))
    peers = sum(1 if cond is None else jnp.where(cond, 1, 0) for cond, where in partners)

    x = x_ref[...].reshape(rows, width).astype(F32)
    a_ref[...] = layer_norm(x, sg_ref[...])

    pl.semaphore_wait(barrier, peers)
    weights = [
        pltpu.make_async_remote_copy(
            src_ref=src, dst_ref=dst, send_sem=wsend.at[k], recv_sem=wrecv.at[k],
            device_id=other, device_id_type=MESH)
        for k, (src, dst) in enumerate([(tq, otq), (tkv, otkv), (to, oto)])
    ]
    for copy in weights[:2]:
        copy.start()

    er = lax.broadcasted_iota(jnp.int32, (TILE, TILE), 0) >> 6
    ec = lax.broadcasted_iota(jnp.int32, (TILE, TILE), 1) >> 6
    ones = jnp.where(er == ec, 1.0, 0.0).astype(BF16)

    def spatial_tile(t, carry):
        c0 = pl.multiple_of(t * TILE, TILE)
        a = a_ref[...]
        q = dot(a, sq[:, pl.ds(c0, TILE)]).astype(BF16).astype(F32)
        k = dot(a, skv[:, pl.ds(c0, TILE)]).astype(BF16).astype(F32)
        v = dot(a, skv[:, pl.ds(pl.multiple_of(width + t * TILE, TILE), TILE)]).astype(BF16).astype(F32)
        prods = jnp.concatenate(
            [q[j * half:(j + 1) * half] * k[i * half:(i + 1) * half]
             for j in range(2) for i in range(2)], axis=0)
        hi = prods.astype(BF16)
        lo = (prods - hi.astype(F32)).astype(BF16)
        s = (dot(hi, ones) + dot(lo, ones)) * 0.125
        for j in range(2):
            s0 = s[(2 * j) * half:(2 * j + 1) * half]
            s1 = s[(2 * j + 1) * half:(2 * j + 2) * half]
            m = jnp.maximum(s0, s1)
            p0 = jnp.exp(s0 - m)
            p1 = jnp.exp(s1 - m)
            total = p0 + p1
            mixed = (p0.astype(BF16).astype(F32) * v[:half] + p1.astype(BF16).astype(F32) * v[half:])
            ctx_ref[pl.ds(j * half, half), pl.ds(c0, TILE)] = (mixed / total).astype(BF16)
        return carry

    lax.fori_loop(0, tiles, spatial_tile, 0, unroll=both_tiles)

    def spatial_out(t, carry):
        c0 = pl.multiple_of(t * TILE, TILE)
        update = dot(ctx_ref[...], so[:, pl.ds(c0, TILE)])
        res = x_ref[:, :, pl.ds(c0, TILE)].astype(F32) + update.reshape(joints, half, TILE)
        sp_ref[:, :, pl.ds(c0, TILE)] = res.astype(BF16)
        return carry

    lax.fori_loop(0, tiles, spatial_out, 0, unroll=2 * both_tiles)
    nb_ref[...] = layer_norm(
        sp_ref[...].reshape(rows, width).astype(F32), tg_ref[...]).reshape(joints, half, width)

    mine = pl.ds(pl.multiple_of(core * half, half), half)
    sends = []

    def send(cond, src, slot, part, sem, where):
        at = pl.ds(pl.multiple_of(part * half, half), half)
        copy = pltpu.make_async_remote_copy(
            src_ref=src, dst_ref=blk.at[slot, at, :], send_sem=sem, recv_sem=recv.at[slot, part],
            device_id=where, device_id_type=MESH)
        guarded(cond, copy.start)
        sends.append((cond, copy))

    fits = me + hop < n
    ahead = both(me + hop)
    send(fits, nb_ref.at[core], hop, core, isend.at[0], ahead[0])
    send(fits, nb_ref.at[1 - core], hop, core, isend.at[1], ahead[1])
    send(None, nb_ref.at[1 - core], 0, core, isend.at[2], other)
    if cols == 2:
        beside = both(mate)
        send(y == 0, nb_ref.at[core], 1, core, isend.at[3], beside[0])
        send(y == 0, nb_ref.at[1 - core], 1, core, isend.at[4], beside[1])
    weights[2].start()
    blk[0, mine, :] = nb_ref[core]

    def arrived(slot, part):
        view = blk.at[slot, pl.ds(pl.multiple_of(part * half, half), half), :]
        pltpu.make_async_copy(view, view, recv.at[slot, part]).wait()

    def forward(slot, part):
        have = me >= slot
        src = blk.at[slot, pl.ds(part * half, half), :]
        if slot % hop == 0 and slot + hop <= window:
            send(have & fits, src, slot + hop, part, zsend.at[slot, part], both(me + hop)[0])
        if cols == 2 and slot % 2 == 0:
            if slot + 1 <= window:
                send(have, src, slot + 1 - 2 * y, part, ysend.at[slot, part], both(mate)[0])
            elif part == 0:
                send(have & (y == 1), src, slot - 1, part, ysend.at[slot, part], both(mate)[0])
        if cols == 2 and slot == window - 3 and part == 1:
            send(have & fits & (y == 0), src, slot + 2, part, zsend.at[slot, part], both(me + hop)[0])

    arrived(0, 1 - core)

    lane = lax.broadcasted_iota(jnp.int32, (1, TILE), 1) >> 6
    pick = [lane == g for g in range(GROUP)]
    wq, wkv = (tq, otq), (tkv, otkv)

    def queries(h):
        def query_tile(t, carry):
            c0 = pl.multiple_of(t * TILE, TILE)
            q = dot(blk[0], wq[h][:, pl.ds(c0, TILE)]).astype(BF16).astype(F32) * 0.125
            for g in range(GROUP):
                qm[h * per_half + t, pl.ds(g * span, span), :] = jnp.where(pick[g], q, 0.0).astype(BF16)
            return carry

        lax.fori_loop(0, per_half, query_tile, 0, unroll=both_tiles)

    query = lax.broadcasted_iota(jnp.int32, (span, span), 0) + me * span
    first = jnp.zeros((span, span), jnp.int32)
    end = jnp.int32(0)
    for c in range(clips):
        end = end + len_ref[c]
        first = jnp.where(query >= end, end, first)
    column = lax.broadcasted_iota(jnp.int32, (span, span), 1)

    def by_head(parts):
        res = parts[GROUP - 1]
        for g in range(GROUP - 2, -1, -1):
            res = jnp.where(pick[g], parts[g], res)
        return res

    def attend(slots, h):
        start = slots[0] == 0
        count = len(slots)

        def shade(slot):
            key = column + (me - slot) * span
            seen = key >= first
            if slot == 0:
                seen = seen & (key <= query)
            return jnp.where(seen, 0.0, -1e30).astype(F32)

        bias = jnp.concatenate([shade(slot) for slot in slots], axis=1)
        bias = jnp.concatenate([bias] * GROUP, axis=0)

        def wide(col):
            return jnp.concatenate([col] * count, axis=1)

        def tile(u, carry):
            t = h * per_half + u
            b = jnp.concatenate([blk[slot] for slot in slots], axis=0)
            c0 = u * TILE
            k = dot(b, wkv[h][:, pl.ds(pl.multiple_of(c0, TILE), TILE)]).astype(BF16)
            v = dot(b, wkv[h][:, pl.ds(pl.multiple_of(width // 2 + c0, TILE), TILE)]).astype(BF16)
            s = lax.dot_general(qm[t], k, (((1,), (1,)), ((), ())), preferred_element_type=F32)
            s = s + bias
            top = jnp.max(s, axis=-1, keepdims=True)
            if start:
                m = jnp.broadcast_to(top, (GROUP * span, span))
            else:
                old = m_ref[t]
                m = jnp.maximum(old, top)
                fade = jnp.exp(old - m)
            p = jnp.exp(s - wide(m))
            total = sum(p[:, z * span:(z + 1) * span] for z in range(count))
            l_ref[t] = total if start else l_ref[t] * fade + total
            m_ref[t] = m
            pv = dot(p.astype(BF16), v)
            new = by_head([pv[g * span:(g + 1) * span] for g in range(GROUP)])
            if start:
                acc_ref[t] = new
            else:
                keep = by_head([jnp.concatenate([fade[g * span:(g + 1) * span]] * 2, axis=1)
                                for g in range(GROUP)])
                acc_ref[t] = acc_ref[t] * keep + new
            return carry

        lax.fori_loop(0, per_half, tile, 0, unroll=both_tiles)

    queries(0)
    attend([0], 0)
    weights[0].wait_recv()
    queries(1)
    weights[1].wait_recv()
    attend([0], 1)

    def take(slot):
        for part in range(2):
            pl.when(me >= slot)(lambda part=part: arrived(slot, part))
            forward(slot, part)

    def use(cond, slots):
        @pl.when(cond)
        def _():
            attend(slots, 0)
            attend(slots, 1)

    if cols == 2 and window == 4:
        take(2)
        use(me >= 2, [2])
        take(1)
        take(4)
        use(me >= 4, [1, 4])
        use((me >= 1) & (me < 4), [1])
        take(3)
        use(me >= 3, [3])
    else:
        for slot in range(1, window + 1):
            take(slot)
            use(me >= slot, [slot])

    def finish(t, carry):
        c0 = pl.multiple_of(t * TILE, TILE)
        total = jnp.sum(l_ref[t], axis=-1, keepdims=True)
        parts = [jnp.broadcast_to(total[g * span:(g + 1) * span], (span, TILE)) for g in range(GROUP)]
        ctx_ref[:, pl.ds(c0, TILE)] = (acc_ref[t] / by_head(parts)).astype(BF16)
        return carry

    lax.fori_loop(0, tiles, finish, 0, unroll=2 * both_tiles)
    weights[2].wait_recv()

    def project(t, carry):
        c0 = pl.multiple_of(t * TILE, TILE)
        hw = width // 2
        res = dot(ctx_ref[:, :hw], to[:, pl.ds(c0, TILE)]) + dot(ctx_ref[:, hw:], oto[:, pl.ds(c0, TILE)])
        out_ref[:, pl.ds(c0, TILE)] = res.astype(BF16)
        return carry

    lax.fori_loop(0, tiles, project, 0, unroll=2 * both_tiles)

    for cond, copy in sends:
        guarded(cond, copy.wait_send)
    for copy in weights:
        copy.wait_send()


def shards(n, cols, motion, s_gain, s_query, s_key_value, s_out, t_gain, t_query, t_key_value, t_out, lengths):
    half, joints, width = motion.shape
    span = 2 * half
    hw = width // 2
    window = n // 2
    tiles = width // TILE
    x = jnp.transpose(motion, (1, 0, 2))
    skv = s_key_value.reshape(width, 2 * width)
    tkv = t_key_value.reshape(width, 2 * hw)
    vmem = pl.BlockSpec(memory_space=pltpu.VMEM)
    sp, out = pl.pallas_call(
        functools.partial(kernel, n, cols, lengths.shape[0]),
        out_shape=(jax.ShapeDtypeStruct((joints, half, width), BF16),
                   jax.ShapeDtypeStruct((span, width), BF16)),
        in_specs=[pl.BlockSpec(memory_space=pltpu.SMEM), vmem, vmem, vmem] + [vmem] * 6,
        out_specs=(vmem, vmem),
        scratch_shapes=[
            pltpu.VMEM((width, hw), BF16),
            pltpu.VMEM((width, 2 * hw), BF16),
            pltpu.VMEM((hw, width), BF16),
            pltpu.VMEM((joints * half, width), BF16),
            pltpu.VMEM((span, width), BF16),
            pltpu.VMEM((joints, half, width), BF16),
            pltpu.VMEM((window + 1, span, width), BF16),
            pltpu.VMEM((tiles, GROUP * span, TILE), BF16),
            pltpu.VMEM((tiles, GROUP * span, span), F32),
            pltpu.VMEM((tiles, GROUP * span, span), F32),
            pltpu.VMEM((tiles, span, TILE), F32),
            pltpu.SemaphoreType.DMA((3,)),
            pltpu.SemaphoreType.DMA((3,)),
            pltpu.SemaphoreType.DMA((5,)),
            pltpu.SemaphoreType.DMA((window + 1, 2)),
            pltpu.SemaphoreType.DMA((window + 1, 2)),
            pltpu.SemaphoreType.DMA((window + 1, 2)),
        ],
        compiler_params=pltpu.CompilerParams(
            collective_id=0, has_side_effects=True, vmem_limit_bytes=36 * 1024 * 1024),
    )(lengths, x, s_gain.reshape(1, width), t_gain.reshape(1, width),
      s_query, skv, s_out, t_query, tkv, t_out)
    return jnp.transpose(sp, (1, 0, 2)), out.reshape(span, 1, width)


def solution(mesh):
    n = mesh.shape["seq"]
    cols = 2 if n == 8 else 1
    in_specs = (
        P(("parts", "seq", "joint"), None, None),
        P(),
        P(),
        P(),
        P(),
        P(),
        P(None, "joint"),
        P(None, None, "joint"),
        P("joint", None),
        P("parts"),
    )
    out_specs = (P(("parts", "seq", "joint"), None, None), P(("parts", "seq"), "joint", None))
    return jax.shard_map(
        functools.partial(shards, n, cols), mesh=mesh, in_specs=in_specs, out_specs=out_specs, check_vma=False)
```

```python
import functools

import jax
import jax.numpy as jnp
from jax import lax
from jax.experimental import pallas as pl
from jax.experimental.pallas import tpu as pltpu
from jax.sharding import PartitionSpec as P

HEAD = 64
TILE = 256
GROUP = TILE // HEAD
MESH = pl.DeviceIdType.MESH
F32 = jnp.float32
BF16 = jnp.bfloat16


def layer_norm(wide, gain):
    mean = jnp.mean(wide, axis=-1, keepdims=True)
    centred = wide - mean
    spread = jnp.mean(centred * centred, axis=-1, keepdims=True)
    return (centred * lax.rsqrt(spread + 1e-05) * gain).astype(BF16)


def dot(a, b):
    return jnp.dot(a, b, preferred_element_type=F32)


def kernel(
    n, cols, clips,
    len_ref, x_ref, sg_ref, tg_ref, sq, skv, so, tq, tkv, to,
    sp_ref, out_ref,
    otq, otkv, oto, a_ref, ctx_ref, nb_ref, blk, qm, m_ref, l_ref, acc_ref,
    wsend, wrecv, isend, zsend, ysend, recv,
):
    joints, half, width = x_ref.shape
    span = 2 * half
    rows = joints * half
    window = n // 2
    tiles = width // TILE
    per_half = tiles // 2
    me = lax.axis_index("seq")
    core = lax.axis_index("joint")
    other = {"joint": 1 - core}

    def both(where):
        return [{"seq": where, "joint": core}, {"seq": where, "joint": 1 - core}]

    hop = cols
    both_tiles = per_half if cols == 2 else 1
    partners = [(None, other)]
    if cols == 2:
        y = lax.rem(me, 2)
        mate = me + 1 - 2 * y
        partners += [(None, dev) for dev in both(mate)]
    partners += [(me + hop < n, dev) for dev in both(me + hop)]
    partners += [(me >= hop, dev) for dev in both(me - hop)]
    barrier = pltpu.get_barrier_semaphore()

    def guarded(cond, action):
        if cond is None:
            action()
        else:
            pl.when(cond)(action)

    for cond, where in partners:
        guarded(cond, lambda where=where: pl.semaphore_signal(
            barrier, inc=1, device_id=where, device_id_type=MESH))
    peers = sum(1 if cond is None else jnp.where(cond, 1, 0) for cond, where in partners)

    x = x_ref[...].reshape(rows, width).astype(F32)
    a_ref[...] = layer_norm(x, sg_ref[...])

    pl.semaphore_wait(barrier, peers)
    weights = [
        pltpu.make_async_remote_copy(
            src_ref=src, dst_ref=dst, send_sem=wsend.at[k], recv_sem=wrecv.at[k],
            device_id=other, device_id_type=MESH)
        for k, (src, dst) in enumerate([(tq, otq), (tkv, otkv), (to, oto)])
    ]
    for copy in weights[:2]:
        copy.start()

    er = lax.broadcasted_iota(jnp.int32, (TILE, TILE), 0) >> 6
    ec = lax.broadcasted_iota(jnp.int32, (TILE, TILE), 1) >> 6
    ones = jnp.where(er == ec, 1.0, 0.0).astype(BF16)

    def spatial_tile(t, carry):
        c0 = pl.multiple_of(t * TILE, TILE)
        a = a_ref[...]
        q = dot(a, sq[:, pl.ds(c0, TILE)]).astype(BF16).astype(F32)
        k = dot(a, skv[:, pl.ds(c0, TILE)]).astype(BF16).astype(F32)
        v = dot(a, skv[:, pl.ds(pl.multiple_of(width + t * TILE, TILE), TILE)]).astype(BF16).astype(F32)
        prods = jnp.concatenate(
            [q[j * half:(j + 1) * half] * k[i * half:(i + 1) * half]
             for j in range(2) for i in range(2)], axis=0)
        hi = prods.astype(BF16)
        lo = (prods - hi.astype(F32)).astype(BF16)
        s = (dot(hi, ones) + dot(lo, ones)) * 0.125
        for j in range(2):
            s0 = s[(2 * j) * half:(2 * j + 1) * half]
            s1 = s[(2 * j + 1) * half:(2 * j + 2) * half]
            m = jnp.maximum(s0, s1)
            p0 = jnp.exp(s0 - m)
            p1 = jnp.exp(s1 - m)
            total = p0 + p1
            mixed = (p0.astype(BF16).astype(F32) * v[:half] + p1.astype(BF16).astype(F32) * v[half:])
            ctx_ref[pl.ds(j * half, half), pl.ds(c0, TILE)] = (mixed / total).astype(BF16)
        return carry

    lax.fori_loop(0, tiles, spatial_tile, 0, unroll=both_tiles)

    def spatial_out(t, carry):
        c0 = pl.multiple_of(t * TILE, TILE)
        update = dot(ctx_ref[...], so[:, pl.ds(c0, TILE)])
        res = x_ref[:, :, pl.ds(c0, TILE)].astype(F32) + update.reshape(joints, half, TILE)
        sp_ref[:, :, pl.ds(c0, TILE)] = res.astype(BF16)
        return carry

    lax.fori_loop(0, tiles, spatial_out, 0, unroll=2 * both_tiles)
    nb_ref[...] = layer_norm(
        sp_ref[...].reshape(rows, width).astype(F32), tg_ref[...]).reshape(joints, half, width)

    mine = pl.ds(pl.multiple_of(core * half, half), half)
    sends = []

    def send(cond, src, slot, part, sem, where):
        at = pl.ds(pl.multiple_of(part * half, half), half)
        copy = pltpu.make_async_remote_copy(
            src_ref=src, dst_ref=blk.at[slot, at, :], send_sem=sem, recv_sem=recv.at[slot, part],
            device_id=where, device_id_type=MESH)
        guarded(cond, copy.start)
        sends.append((cond, copy))

    fits = me + hop < n
    ahead = both(me + hop)
    send(fits, nb_ref.at[core], hop, core, isend.at[0], ahead[0])
    if cols == 2:
        beside = both(mate)
        send(y == 0, nb_ref.at[core], 1, core, isend.at[3], beside[0])
    send(None, nb_ref.at[1 - core], 0, core, isend.at[2], other)
    blk[0, mine, :] = nb_ref[core]

    def arrived(slot, part):
        view = blk.at[slot, pl.ds(pl.multiple_of(part * half, half), half), :]
        pltpu.make_async_copy(view, view, recv.at[slot, part]).wait()

    def forward(slot, turn):
        have = me >= slot
        part = core if turn == 0 else 1 - core
        src = blk.at[slot, pl.ds(pl.multiple_of(part * half, half), half), :]
        if slot % hop == 0 and slot + hop <= window:
            send(have & fits, src, slot + hop, part, zsend.at[slot, turn], both(me + hop)[0])
        if cols == 2 and slot % 2 == 0:
            if slot + 1 <= window:
                send(have, src, slot + 1 - 2 * y, part, ysend.at[slot, turn], both(mate)[0])
            elif turn == 0:
                send(have & (y == 1), src, slot - 1, part, ysend.at[slot, turn], both(mate)[0])
        if cols == 2 and slot == window - 3 and turn == 1:
            send(have & fits & (y == 0), src, slot + 2, part, zsend.at[slot, turn], both(me + hop)[0])

    arrived(0, 1 - core)

    lane = lax.broadcasted_iota(jnp.int32, (1, TILE), 1) >> 6
    pick = [lane == g for g in range(GROUP)]
    wq, wkv = (tq, otq), (tkv, otkv)

    def queries(h):
        def query_tile(t, carry):
            c0 = pl.multiple_of(t * TILE, TILE)
            q = dot(blk[0], wq[h][:, pl.ds(c0, TILE)]).astype(BF16).astype(F32) * 0.125
            for g in range(GROUP):
                qm[h * per_half + t, pl.ds(g * span, span), :] = jnp.where(pick[g], q, 0.0).astype(BF16)
            return carry

        lax.fori_loop(0, per_half, query_tile, 0, unroll=both_tiles)

    query = lax.broadcasted_iota(jnp.int32, (span, span), 0) + me * span
    first = jnp.zeros((span, span), jnp.int32)
    end = jnp.int32(0)
    for c in range(clips):
        end = end + len_ref[c]
        first = jnp.where(query >= end, end, first)
    column = lax.broadcasted_iota(jnp.int32, (span, span), 1)

    def by_head(parts):
        res = parts[GROUP - 1]
        for g in range(GROUP - 2, -1, -1):
            res = jnp.where(pick[g], parts[g], res)
        return res

    def attend(slots, h):
        start = slots[0] == 0
        count = len(slots)

        def shade(slot):
            key = column + (me - slot) * span
            seen = key >= first
            if slot == 0:
                seen = seen & (key <= query)
            return jnp.where(seen, 0.0, -1e30).astype(F32)

        bias = jnp.concatenate([shade(slot) for slot in slots], axis=1)
        bias = jnp.concatenate([bias] * GROUP, axis=0)

        def wide(col):
            return jnp.concatenate([col] * count, axis=1)

        def tile(u, carry):
            t = h * per_half + u
            b = jnp.concatenate([blk[slot] for slot in slots], axis=0)
            c0 = u * TILE
            k = dot(b, wkv[h][:, pl.ds(pl.multiple_of(c0, TILE), TILE)]).astype(BF16)
            v = dot(b, wkv[h][:, pl.ds(pl.multiple_of(width // 2 + c0, TILE), TILE)]).astype(BF16)
            s = lax.dot_general(qm[t], k, (((1,), (1,)), ((), ())), preferred_element_type=F32)
            s = s + bias
            top = jnp.max(s, axis=-1, keepdims=True)
            if start:
                m = jnp.broadcast_to(top, (GROUP * span, span))
            else:
                old = m_ref[t]
                m = jnp.maximum(old, top)
                fade = jnp.exp(old - m)
            p = jnp.exp(s - wide(m))
            total = sum(p[:, z * span:(z + 1) * span] for z in range(count))
            l_ref[t] = total if start else l_ref[t] * fade + total
            m_ref[t] = m
            pv = dot(p.astype(BF16), v)
            new = by_head([pv[g * span:(g + 1) * span] for g in range(GROUP)])
            if start:
                acc_ref[t] = new
            else:
                keep = by_head([jnp.concatenate([fade[g * span:(g + 1) * span]] * 2, axis=1)
                                for g in range(GROUP)])
                acc_ref[t] = acc_ref[t] * keep + new
            return carry

        lax.fori_loop(0, per_half, tile, 0, unroll=both_tiles)

    queries(0)
    send(fits, nb_ref.at[1 - core], hop, core, isend.at[1], ahead[1])
    if cols == 2:
        send(y == 0, nb_ref.at[1 - core], 1, core, isend.at[4], beside[1])
    weights[2].start()
    attend([0], 0)
    weights[0].wait_recv()
    queries(1)
    weights[1].wait_recv()
    attend([0], 1)

    def take(slot):
        for turn, part in enumerate((core, 1 - core)):
            pl.when(me >= slot)(lambda part=part: arrived(slot, part))
            forward(slot, turn)

    def use(cond, slots):
        @pl.when(cond)
        def _():
            attend(slots, 0)
            attend(slots, 1)

    if cols == 2 and window == 4:
        take(2)
        use(me >= 2, [2])
        take(1)
        take(4)
        use(me >= 4, [1, 4])
        use((me >= 1) & (me < 4), [1])
        take(3)
        use(me >= 3, [3])
    else:
        for slot in range(1, window + 1):
            take(slot)
            use(me >= slot, [slot])

    def finish(t, carry):
        c0 = pl.multiple_of(t * TILE, TILE)
        total = jnp.sum(l_ref[t], axis=-1, keepdims=True)
        parts = [jnp.broadcast_to(total[g * span:(g + 1) * span], (span, TILE)) for g in range(GROUP)]
        ctx_ref[:, pl.ds(c0, TILE)] = (acc_ref[t] / by_head(parts)).astype(BF16)
        return carry

    lax.fori_loop(0, tiles, finish, 0, unroll=2 * both_tiles)
    weights[2].wait_recv()

    def project(t, carry):
        c0 = pl.multiple_of(t * TILE, TILE)
        hw = width // 2
        res = dot(ctx_ref[:, :hw], to[:, pl.ds(c0, TILE)]) + dot(ctx_ref[:, hw:], oto[:, pl.ds(c0, TILE)])
        out_ref[:, pl.ds(c0, TILE)] = res.astype(BF16)
        return carry

    lax.fori_loop(0, tiles, project, 0, unroll=2 * both_tiles)

    for cond, copy in sends:
        guarded(cond, copy.wait_send)
    for copy in weights:
        copy.wait_send()


def shards(n, cols, motion, s_gain, s_query, s_key_value, s_out, t_gain, t_query, t_key_value, t_out, lengths):
    half, joints, width = motion.shape
    span = 2 * half
    hw = width // 2
    window = n // 2
    tiles = width // TILE
    x = jnp.transpose(motion, (1, 0, 2))
    skv = s_key_value.reshape(width, 2 * width)
    tkv = t_key_value.reshape(width, 2 * hw)
    vmem = pl.BlockSpec(memory_space=pltpu.VMEM)
    sp, out = pl.pallas_call(
        functools.partial(kernel, n, cols, lengths.shape[0]),
        out_shape=(jax.ShapeDtypeStruct((joints, half, width), BF16),
                   jax.ShapeDtypeStruct((span, width), BF16)),
        in_specs=[pl.BlockSpec(memory_space=pltpu.SMEM), vmem, vmem, vmem] + [vmem] * 6,
        out_specs=(vmem, vmem),
        scratch_shapes=[
            pltpu.VMEM((width, hw), BF16),
            pltpu.VMEM((width, 2 * hw), BF16),
            pltpu.VMEM((hw, width), BF16),
            pltpu.VMEM((joints * half, width), BF16),
            pltpu.VMEM((span, width), BF16),
            pltpu.VMEM((joints, half, width), BF16),
            pltpu.VMEM((window + 1, span, width), BF16),
            pltpu.VMEM((tiles, GROUP * span, TILE), BF16),
            pltpu.VMEM((tiles, GROUP * span, span), F32),
            pltpu.VMEM((tiles, GROUP * span, span), F32),
            pltpu.VMEM((tiles, span, TILE), F32),
            pltpu.SemaphoreType.DMA((3,)),
            pltpu.SemaphoreType.DMA((3,)),
            pltpu.SemaphoreType.DMA((5,)),
            pltpu.SemaphoreType.DMA((window + 1, 2)),
            pltpu.SemaphoreType.DMA((window + 1, 2)),
            pltpu.SemaphoreType.DMA((window + 1, 2)),
        ],
        compiler_params=pltpu.CompilerParams(
            collective_id=0, has_side_effects=True, vmem_limit_bytes=36 * 1024 * 1024),
    )(lengths, x, s_gain.reshape(1, width), t_gain.reshape(1, width),
      s_query, skv, s_out, t_query, tkv, t_out)
    return jnp.transpose(sp, (1, 0, 2)), out.reshape(span, 1, width)


def solution(mesh):
    n = mesh.shape["seq"]
    cols = 2 if n == 8 else 1
    in_specs = (
        P(("parts", "seq", "joint"), None, None),
        P(),
        P(),
        P(),
        P(),
        P(),
        P(None, "joint"),
        P(None, None, "joint"),
        P("joint", None),
        P("parts"),
    )
    out_specs = (P(("parts", "seq", "joint"), None, None), P(("parts", "seq"), "joint", None))
    return jax.shard_map(
        functools.partial(shards, n, cols), mesh=mesh, in_specs=in_specs, out_specs=out_specs, check_vma=False)
```

```python
import functools

import jax
import jax.numpy as jnp
from jax import lax
from jax.experimental import pallas as pl
from jax.experimental.pallas import tpu as pltpu
from jax.sharding import PartitionSpec as P

HEAD = 64
TILE = 256
GROUP = TILE // HEAD
MESH = pl.DeviceIdType.MESH
F32 = jnp.float32
BF16 = jnp.bfloat16


def layer_norm(wide, gain):
    mean = jnp.mean(wide, axis=-1, keepdims=True)
    centred = wide - mean
    spread = jnp.mean(centred * centred, axis=-1, keepdims=True)
    return (centred * lax.rsqrt(spread + 1e-05) * gain).astype(BF16)


def dot(a, b):
    return jnp.dot(a, b, preferred_element_type=F32)


def kernel(
    n, cols, clips,
    len_ref, x_ref, sg_ref, tg_ref, sq, skv, so, tq, tkv, to,
    sp_ref, out_ref,
    otq, otkv, oto, a_ref, ctx_ref, nb_ref, blk, qm, m_ref, l_ref, acc_ref,
    wsend, wrecv, isend, zsend, ysend, recv,
):
    joints, half, width = x_ref.shape
    span = 2 * half
    rows = joints * half
    window = n // 2
    tiles = width // TILE
    per_half = tiles // 2
    me = lax.axis_index("seq")
    core = lax.axis_index("joint")
    other = {"joint": 1 - core}

    def both(where):
        return [{"seq": where, "joint": core}, {"seq": where, "joint": 1 - core}]

    hop = cols
    both_tiles = per_half if cols == 2 else 1
    partners = [(None, other)]
    if cols == 2:
        y = lax.rem(me, 2)
        mate = me + 1 - 2 * y
        partners += [(None, dev) for dev in both(mate)]
    partners += [(me + hop < n, dev) for dev in both(me + hop)]
    partners += [(me >= hop, dev) for dev in both(me - hop)]
    barrier = pltpu.get_barrier_semaphore()

    def guarded(cond, action):
        if cond is None:
            action()
        else:
            pl.when(cond)(action)

    for cond, where in partners:
        guarded(cond, lambda where=where: pl.semaphore_signal(
            barrier, inc=1, device_id=where, device_id_type=MESH))
    peers = sum(1 if cond is None else jnp.where(cond, 1, 0) for cond, where in partners)

    x = x_ref[...].reshape(rows, width).astype(F32)
    a_ref[...] = layer_norm(x, sg_ref[...])

    pl.semaphore_wait(barrier, peers)
    weights = [
        pltpu.make_async_remote_copy(
            src_ref=src, dst_ref=dst, send_sem=wsend.at[k], recv_sem=wrecv.at[k],
            device_id=other, device_id_type=MESH)
        for k, (src, dst) in enumerate([(tq, otq), (tkv, otkv), (to, oto)])
    ]
    for copy in weights[:2]:
        copy.start()

    er = lax.broadcasted_iota(jnp.int32, (TILE, TILE), 0) >> 6
    ec = lax.broadcasted_iota(jnp.int32, (TILE, TILE), 1) >> 6
    ones = jnp.where(er == ec, 1.0, 0.0).astype(BF16)

    def spatial_tile(t, carry):
        c0 = pl.multiple_of(t * TILE, TILE)
        a = a_ref[...]
        q = dot(a, sq[:, pl.ds(c0, TILE)]).astype(BF16).astype(F32)
        k = dot(a, skv[:, pl.ds(c0, TILE)]).astype(BF16).astype(F32)
        v = dot(a, skv[:, pl.ds(pl.multiple_of(width + t * TILE, TILE), TILE)]).astype(BF16).astype(F32)
        prods = jnp.concatenate(
            [q[j * half:(j + 1) * half] * k[i * half:(i + 1) * half]
             for j in range(2) for i in range(2)], axis=0)
        hi = prods.astype(BF16)
        lo = (prods - hi.astype(F32)).astype(BF16)
        s = (dot(hi, ones) + dot(lo, ones)) * 0.125
        for j in range(2):
            s0 = s[(2 * j) * half:(2 * j + 1) * half]
            s1 = s[(2 * j + 1) * half:(2 * j + 2) * half]
            m = jnp.maximum(s0, s1)
            p0 = jnp.exp(s0 - m)
            p1 = jnp.exp(s1 - m)
            total = p0 + p1
            mixed = (p0.astype(BF16).astype(F32) * v[:half] + p1.astype(BF16).astype(F32) * v[half:])
            ctx_ref[pl.ds(j * half, half), pl.ds(c0, TILE)] = (mixed / total).astype(BF16)
        return carry

    lax.fori_loop(0, tiles, spatial_tile, 0, unroll=2 * both_tiles)

    def spatial_out(t, carry):
        c0 = pl.multiple_of(t * TILE, TILE)
        update = dot(ctx_ref[...], so[:, pl.ds(c0, TILE)])
        res = x_ref[:, :, pl.ds(c0, TILE)].astype(F32) + update.reshape(joints, half, TILE)
        sp_ref[:, :, pl.ds(c0, TILE)] = res.astype(BF16)
        return carry

    lax.fori_loop(0, tiles, spatial_out, 0, unroll=2 * both_tiles)
    nb_ref[...] = layer_norm(
        sp_ref[...].reshape(rows, width).astype(F32), tg_ref[...]).reshape(joints, half, width)

    mine = pl.ds(pl.multiple_of(core * half, half), half)
    sends = []

    def send(cond, src, slot, part, sem, where):
        at = pl.ds(pl.multiple_of(part * half, half), half)
        copy = pltpu.make_async_remote_copy(
            src_ref=src, dst_ref=blk.at[slot, at, :], send_sem=sem, recv_sem=recv.at[slot, part],
            device_id=where, device_id_type=MESH)
        guarded(cond, copy.start)
        sends.append((cond, copy))

    fits = me + hop < n
    ahead = both(me + hop)
    send(fits, nb_ref.at[core], hop, core, isend.at[0], ahead[0])
    if cols == 2:
        beside = both(mate)
        send(y == 0, nb_ref.at[core], 1, core, isend.at[3], beside[0])
    send(None, nb_ref.at[1 - core], 0, core, isend.at[2], other)
    blk[0, mine, :] = nb_ref[core]

    def arrived(slot, part):
        view = blk.at[slot, pl.ds(pl.multiple_of(part * half, half), half), :]
        pltpu.make_async_copy(view, view, recv.at[slot, part]).wait()

    def forward(slot, turn):
        have = me >= slot
        part = core if turn == 0 else 1 - core
        src = blk.at[slot, pl.ds(pl.multiple_of(part * half, half), half), :]
        if slot % hop == 0 and slot + hop <= window:
            send(have & fits, src, slot + hop, part, zsend.at[slot, turn], both(me + hop)[0])
        if cols == 2 and slot % 2 == 0:
            if slot + 1 <= window:
                send(have, src, slot + 1 - 2 * y, part, ysend.at[slot, turn], both(mate)[0])
            elif turn == 0:
                send(have & (y == 1), src, slot - 1, part, ysend.at[slot, turn], both(mate)[0])
        if cols == 2 and slot == window - 3 and turn == 1:
            send(have & fits & (y == 0), src, slot + 2, part, zsend.at[slot, turn], both(me + hop)[0])

    arrived(0, 1 - core)

    lane = lax.broadcasted_iota(jnp.int32, (1, TILE), 1) >> 6
    pick = [lane == g for g in range(GROUP)]
    wq, wkv = (tq, otq), (tkv, otkv)

    def queries(h):
        def query_tile(t, carry):
            c0 = pl.multiple_of(t * TILE, TILE)
            q = dot(blk[0], wq[h][:, pl.ds(c0, TILE)]).astype(BF16).astype(F32) * 0.125
            for g in range(GROUP):
                qm[h * per_half + t, pl.ds(g * span, span), :] = jnp.where(pick[g], q, 0.0).astype(BF16)
            return carry

        lax.fori_loop(0, per_half, query_tile, 0, unroll=both_tiles)

    query = lax.broadcasted_iota(jnp.int32, (span, span), 0) + me * span
    first = jnp.zeros((span, span), jnp.int32)
    end = jnp.int32(0)
    for c in range(clips):
        end = end + len_ref[c]
        first = jnp.where(query >= end, end, first)
    column = lax.broadcasted_iota(jnp.int32, (span, span), 1)

    def by_head(parts):
        res = parts[GROUP - 1]
        for g in range(GROUP - 2, -1, -1):
            res = jnp.where(pick[g], parts[g], res)
        return res

    def attend(slots, h):
        start = slots[0] == 0
        count = len(slots)

        def shade(slot):
            key = column + (me - slot) * span
            seen = key >= first
            if slot == 0:
                seen = seen & (key <= query)
            return jnp.where(seen, 0.0, -1e30).astype(F32)

        bias = jnp.concatenate([shade(slot) for slot in slots], axis=1)
        bias = jnp.concatenate([bias] * GROUP, axis=0)

        def wide(col):
            return jnp.concatenate([col] * count, axis=1)

        def tile(u, carry):
            t = h * per_half + u
            b = jnp.concatenate([blk[slot] for slot in slots], axis=0)
            c0 = u * TILE
            k = dot(b, wkv[h][:, pl.ds(pl.multiple_of(c0, TILE), TILE)]).astype(BF16)
            v = dot(b, wkv[h][:, pl.ds(pl.multiple_of(width // 2 + c0, TILE), TILE)]).astype(BF16)
            s = lax.dot_general(qm[t], k, (((1,), (1,)), ((), ())), preferred_element_type=F32)
            s = s + bias
            top = jnp.max(s, axis=-1, keepdims=True)
            if start:
                m = jnp.broadcast_to(top, (GROUP * span, span))
            else:
                old = m_ref[t]
                m = jnp.maximum(old, top)
                fade = jnp.exp(old - m)
            p = jnp.exp(s - wide(m))
            total = sum(p[:, z * span:(z + 1) * span] for z in range(count))
            l_ref[t] = total if start else l_ref[t] * fade + total
            m_ref[t] = m
            pv = dot(p.astype(BF16), v)
            new = by_head([pv[g * span:(g + 1) * span] for g in range(GROUP)])
            if start:
                acc_ref[t] = new
            else:
                keep = by_head([jnp.concatenate([fade[g * span:(g + 1) * span]] * 2, axis=1)
                                for g in range(GROUP)])
                acc_ref[t] = acc_ref[t] * keep + new
            return carry

        lax.fori_loop(0, per_half, tile, 0, unroll=both_tiles)

    queries(0)
    send(fits, nb_ref.at[1 - core], hop, core, isend.at[1], ahead[1])
    if cols == 2:
        send(y == 0, nb_ref.at[1 - core], 1, core, isend.at[4], beside[1])
    weights[2].start()
    attend([0], 0)
    weights[0].wait_recv()
    queries(1)
    weights[1].wait_recv()
    attend([0], 1)

    def take(slot):
        for turn, part in enumerate((core, 1 - core)):
            pl.when(me >= slot)(lambda part=part: arrived(slot, part))
            forward(slot, turn)

    def use(cond, slots):
        @pl.when(cond)
        def _():
            attend(slots, 0)
            attend(slots, 1)

    if cols == 2 and window == 4:
        take(2)
        use(me >= 2, [2])
        take(1)
        take(4)
        use(me >= 4, [1, 4])
        use((me >= 1) & (me < 4), [1])
        take(3)
        use(me >= 3, [3])
    else:
        for slot in range(1, window + 1):
            take(slot)
            use(me >= slot, [slot])

    def finish(t, carry):
        c0 = pl.multiple_of(t * TILE, TILE)
        total = jnp.sum(l_ref[t], axis=-1, keepdims=True)
        parts = [jnp.broadcast_to(total[g * span:(g + 1) * span], (span, TILE)) for g in range(GROUP)]
        ctx_ref[:, pl.ds(c0, TILE)] = (acc_ref[t] / by_head(parts)).astype(BF16)
        return carry

    lax.fori_loop(0, tiles, finish, 0, unroll=2 * both_tiles)
    weights[2].wait_recv()

    def project(t, carry):
        c0 = pl.multiple_of(t * TILE, TILE)
        hw = width // 2
        res = dot(ctx_ref[:, :hw], to[:, pl.ds(c0, TILE)]) + dot(ctx_ref[:, hw:], oto[:, pl.ds(c0, TILE)])
        out_ref[:, pl.ds(c0, TILE)] = res.astype(BF16)
        return carry

    lax.fori_loop(0, tiles, project, 0, unroll=2 * both_tiles)

    for cond, copy in sends:
        guarded(cond, copy.wait_send)
    for copy in weights:
        copy.wait_send()


def shards(n, cols, motion, s_gain, s_query, s_key_value, s_out, t_gain, t_query, t_key_value, t_out, lengths):
    half, joints, width = motion.shape
    span = 2 * half
    hw = width // 2
    window = n // 2
    tiles = width // TILE
    x = jnp.transpose(motion, (1, 0, 2))
    skv = s_key_value.reshape(width, 2 * width)
    tkv = t_key_value.reshape(width, 2 * hw)
    vmem = pl.BlockSpec(memory_space=pltpu.VMEM)
    sp, out = pl.pallas_call(
        functools.partial(kernel, n, cols, lengths.shape[0]),
        out_shape=(jax.ShapeDtypeStruct((joints, half, width), BF16),
                   jax.ShapeDtypeStruct((span, width), BF16)),
        in_specs=[pl.BlockSpec(memory_space=pltpu.SMEM), vmem, vmem, vmem] + [vmem] * 6,
        out_specs=(vmem, vmem),
        scratch_shapes=[
            pltpu.VMEM((width, hw), BF16),
            pltpu.VMEM((width, 2 * hw), BF16),
            pltpu.VMEM((hw, width), BF16),
            pltpu.VMEM((joints * half, width), BF16),
            pltpu.VMEM((span, width), BF16),
            pltpu.VMEM((joints, half, width), BF16),
            pltpu.VMEM((window + 1, span, width), BF16),
            pltpu.VMEM((tiles, GROUP * span, TILE), BF16),
            pltpu.VMEM((tiles, GROUP * span, span), F32),
            pltpu.VMEM((tiles, GROUP * span, span), F32),
            pltpu.VMEM((tiles, span, TILE), F32),
            pltpu.SemaphoreType.DMA((3,)),
            pltpu.SemaphoreType.DMA((3,)),
            pltpu.SemaphoreType.DMA((5,)),
            pltpu.SemaphoreType.DMA((window + 1, 2)),
            pltpu.SemaphoreType.DMA((window + 1, 2)),
            pltpu.SemaphoreType.DMA((window + 1, 2)),
        ],
        compiler_params=pltpu.CompilerParams(
            collective_id=0, has_side_effects=True, vmem_limit_bytes=36 * 1024 * 1024),
    )(lengths, x, s_gain.reshape(1, width), t_gain.reshape(1, width),
      s_query, skv, s_out, t_query, tkv, t_out)
    return jnp.transpose(sp, (1, 0, 2)), out.reshape(span, 1, width)


def solution(mesh):
    n = mesh.shape["seq"]
    cols = 2 if n == 8 else 1
    in_specs = (
        P(("parts", "seq", "joint"), None, None),
        P(),
        P(),
        P(),
        P(),
        P(),
        P(None, "joint"),
        P(None, None, "joint"),
        P("joint", None),
        P("parts"),
    )
    out_specs = (P(("parts", "seq", "joint"), None, None), P(("parts", "seq"), "joint", None))
    return jax.shard_map(
        functools.partial(shards, n, cols), mesh=mesh, in_specs=in_specs, out_specs=out_specs, check_vma=False)
```
